32 devices in a mesh: grp: 2 (over y), wide: 4 (over z), slc: 2 (over x), sub: 2 (over core).
Axes of the slice: x: 2, y: 2, z: 4, core: 2. Of those that a mesh axis runs over, the one named last changes fastest.
Arguments:
- a_stem: bfloat16 [2, 16, 2048, 256], P(None, ('grp', 'slc', 'sub'), 'wide'), parts along dimension 1, may hold values from -6 to 6
- b_stem: bfloat16 [2, 16, 256, 512], P(None, ('grp', 'slc', 'sub')), parts along dimension 1, may hold values from -0.09375 to 0.09375
- gate_pick: int32 [40], P('grp'), parts along dimension 0, may hold values from 0 to 2
- leg_order: int32 [18], P('grp'), parts along dimension 0, may hold values from 0 to 8, each once
Outputs:
- amplitudes: float32 [2, 8, 4, 4, 32, 512], P(None, 'grp', ('slc', 'sub'), 'wide'), parts along dimension 1
The draws below stay inside these ranges and needn't reach their ends.
There are 2 independent parts, one for each index of `grp`. The reference program is written for one: setup_inputs(seed, part) draws one part's arguments, and reference() takes and returns one part's arrays. A program takes and returns all parts, laid end to end along the dimension named above; each array names one. Nothing has to cross between parts.
Inputs may be any that keep to these rules, and one draw needn't show every extreme that they name: `gate_pick`: an index into the three gates of the steps. `leg_order`: each column leg once.
All inputs are finite; a program needn't handle non-finite values.
Results may differ from the reference program's by a relative error of at most 0.0003.
Values sent between devices are 32-bit elements; how exact they have to be, the bound alone decides.
A program may use at most 320 MiB of HBM per device.

```python
import jax
import jax.numpy as jnp
from jax import lax

CBITS = 9
COLS = 512
K = 256
RLOC = 128
SLICES = 8
ROWS = 2048
QUBITS = 20
N_WIDE = 4
N_SLC = 2
N_SUB = 2


def place_ends(values, key, least, high):
    shape = values.shape
    place = [jax.random.randint(jax.random.fold_in(key, axis), (), 0, shape[axis]) for axis in range(len(shape))]
    values = values.at[tuple(place)].set(least)
    longest = shape.index(max(shape))
    place[longest] = (place[longest] + 1) % shape[longest]
    return values.at[tuple(place)].set(high)


def block_levels(key, extent, split, low, high):
    def one(dim, parts):
        heights = jax.random.uniform(jax.random.fold_in(jax.random.fold_in(key, 6), dim), (parts,), jnp.float32, low / len(split), high / len(split))
        return jnp.repeat(jnp.exp(heights), extent[dim] // parts).reshape((-1,) + (1,) * (len(extent) - dim - 1))

    gain = one(*split[0])
    for cut in split[1:]:
        gain = gain * one(*cut)
    return gain


def scatter_about(stream_key, shape, scale, bound, split=(), kind=jnp.bfloat16):
    values = scale * jax.random.normal(stream_key, shape, jnp.float32)
    if split:
        values = values * block_levels(stream_key, shape, split, -0.22, 0.18)
    return jnp.clip(values, -bound, bound).astype(kind)


def setup_inputs(seed: int = 0, part: int = 0) -> dict:
    streams_of = jax.random.split(jax.random.key(seed), 5)
    own_keys = jax.random.split(jax.random.fold_in(streams_of[4], part), 5)
    return {
        "a_stem": scatter_about(own_keys[0], (2, SLICES, ROWS, K), 1.0, 6.0, ((1, 4), (2, 4))),
        "b_stem": scatter_about(own_keys[1], (2, SLICES, K, COLS), (2 * K * SLICES) ** -0.5, 0.09375, ((1, 4),)),
        "gate_pick": place_ends(jax.random.randint(own_keys[2], (QUBITS,), 0, 3), jax.random.fold_in(own_keys[2], 1), 0, 2).astype(jnp.int32),
        "leg_order": jax.random.permutation(own_keys[3], CBITS).astype(jnp.int32),
    }


HALF_ROOT = 0.7071067811865476
GATE_REAL = (((HALF_ROOT, 0.0), (0.0, HALF_ROOT)), ((HALF_ROOT, -HALF_ROOT), (HALF_ROOT, HALF_ROOT)), ((HALF_ROOT, -0.5), (0.5, HALF_ROOT)))
GATE_IMAG = (((0.0, -HALF_ROOT), (-HALF_ROOT, 0.0)), ((0.0, 0.0), (0.0, 0.0)), ((0.0, -0.5), (-0.5, 0.0)))


def leg_apply(matrix, field, axis_pos):
    moved = jnp.tensordot(matrix, field, axes=((1,), (axis_pos,)), precision=lax.Precision.HIGHEST)
    return jnp.moveaxis(moved, 0, axis_pos)


def reference(a_stem, b_stem, gate_pick, leg_order):
    high = lax.Precision.HIGHEST
    a_slices = jnp.moveaxis(a_stem, 1, 0)
    b_slices = jnp.moveaxis(b_stem, 1, 0)
    zeros = jnp.zeros((ROWS, COLS), jnp.float32)

    def add_slice(totals, stem_pair):
        a_part = stem_pair[0].astype(jnp.float32)
        b_part = stem_pair[1].astype(jnp.float32)
        real_part = jnp.dot(a_part[0], b_part[0], precision=high) - jnp.dot(a_part[1], b_part[1], precision=high)
        imag_part = jnp.dot(a_part[0], b_part[1], precision=high) + jnp.dot(a_part[1], b_part[0], precision=high)
        return (totals[0] + real_part, totals[1] + imag_part), None

    (real_sum, imag_sum), unused = lax.scan(add_slice, (zeros, zeros), (a_slices, b_slices))
    table_real = jnp.array(GATE_REAL, jnp.float32)
    table_imag = jnp.array(GATE_IMAG, jnp.float32)
    leg_shape = (2,) * QUBITS
    real_field = real_sum.reshape(leg_shape)
    imag_field = imag_sum.reshape(leg_shape)
    for leg_pos in range(QUBITS):
        u_real = table_real[gate_pick[leg_pos]]
        u_imag = table_imag[gate_pick[leg_pos]]
        new_real = leg_apply(u_real, real_field, leg_pos) - leg_apply(u_imag, imag_field, leg_pos)
        new_imag = leg_apply(u_real, imag_field, leg_pos) + leg_apply(u_imag, real_field, leg_pos)
        real_field = new_real
        imag_field = new_imag
    positions = jnp.arange(COLS, dtype=jnp.int32)
    source = jnp.zeros((COLS,), jnp.int32)
    for out_bit in range(CBITS):
        source = source + (((positions >> out_bit) & 1) << leg_order[out_bit])
    real_out = jnp.take(real_field.reshape(ROWS, COLS), source, axis=1)
    imag_out = jnp.take(imag_field.reshape(ROWS, COLS), source, axis=1)
    stacked = jnp.stack((real_out, imag_out), 0)
    return stacked.reshape(2, N_WIDE, N_SLC * N_SUB, N_WIDE, RLOC // N_WIDE, COLS)
```

```python
import functools

import jax
import jax.numpy as jnp
from jax import lax
from jax.experimental import pallas as pl
from jax.experimental.pallas import tpu as pltpu
from jax.sharding import PartitionSpec as P

HALF_ROOT = 0.7071067811865476
MESH = pl.DeviceIdType.MESH


def eighth_turns(pick):
    return jnp.where(pick == 0, 2, jnp.where(pick == 2, 1, 0)).astype(jnp.int32)


def bit_of(value, position):
    return lax.shift_right_logical(value, jnp.full_like(value, position)) & 1


def turn_cos(turns):
    angle = turns & 7
    size = jnp.where((angle & 1) == 1, HALF_ROOT, jnp.where((angle & 2) == 0, 1.0, 0.0))
    return jnp.where(((angle + 2) & 4) == 4, -size, size).astype(jnp.float32)


def turn_sin(turns):
    return turn_cos(turns + 6)


def sign_of(target, source):
    value = (~target) & source
    for step in (8, 4, 2, 1):
        value = value ^ lax.shift_right_logical(value, jnp.full_like(value, step))
    return (1 - 2 * (value & 1)).astype(jnp.float32)


def butterfly(blocks):
    count = len(blocks)
    mask = 1
    while mask < count:
        mixed = list(blocks)
        for index in range(count):
            if not index & mask:
                low, high = blocks[index], blocks[index | mask]
                mixed[index] = low - high
                mixed[index | mask] = low + high
        blocks = mixed
        mask *= 2
    return blocks


def split_two(value):
    top = value.astype(jnp.bfloat16)
    rest = (value - top.astype(jnp.float32)).astype(jnp.bfloat16)
    return top, rest


def kernel_body(
    dims,
    pick_ref, order_ref, a_hbm, b_hbm, out_ref,
    a_vm, b_vm, row_cos, row_sin, row_mat, col_mat, out_cos, out_sin,
    sub_out, sub_in, slc_out, slc_in, wide_out, wide_in, acc,
    a_sem, b_sem, sub_ss, sub_rs, slc_ss, slc_rs, wide_ss, wide_rs,
):
    (n_sub, n_slc, n_wide, slices, rows_loc, loc, loc_pad, columns, width) = dims
    f32 = jnp.float32
    i32 = jnp.int32
    group = n_sub * n_slc
    chunks = columns // width
    col_bits = columns.bit_length() - 1
    wide_bits = n_wide.bit_length() - 1
    group_bits = group.bit_length() - 1
    rows_bits = rows_loc.bit_length() - 1
    loc_bits = loc.bit_length() - 1
    row_bits = wide_bits + group_bits + rows_bits
    me_sub = lax.axis_index("sub")
    me_slc = lax.axis_index("slc")
    me_wide = lax.axis_index("wide")
    me_group = me_slc * n_sub + me_sub

    a_copy = pltpu.make_async_copy(a_hbm, a_vm, a_sem)
    b_copies = [
        pltpu.make_async_copy(
            b_hbm.at[:, :, :, pl.ds(c * width, width)], b_vm.at[c], b_sem.at[c]
        )
        for c in range(chunks)
    ]
    b_copies[0].start()
    a_copy.start()
    for c in range(1, chunks):
        b_copies[c].start()

    barrier = pltpu.get_barrier_semaphore()
    for axis, me, count in (("sub", me_sub, n_sub), ("slc", me_slc, n_slc), ("wide", me_wide, n_wide)):
        for k in range(1, count):
            pl.semaphore_signal(
                barrier, inc=1, device_id={axis: lax.rem(me + k, count)}, device_id_type=MESH
            )

    turns = [eighth_turns(pick_ref[q]) for q in range(row_bits + col_bits)]

    def scalar_turns(value, first, count):
        total = jnp.int32(0)
        for j in range(count):
            total = total + turns[first + count - 1 - j] * (lax.shift_right_logical(value, jnp.int32(j)) & 1)
        return total

    def vector_turns(value, first, count):
        total = jnp.zeros_like(value)
        for j in range(count):
            total = total + turns[first + count - 1 - j] * bit_of(value, j)
        return total

    row_iota = lax.broadcasted_iota(i32, (rows_loc, 128), 0)
    row_turns = vector_turns(row_iota, wide_bits + group_bits, rows_bits)
    row_turns = row_turns + scalar_turns(me_wide.astype(i32), 0, wide_bits)
    for s in range(group):
        here = row_turns + scalar_turns(jnp.int32(s), wide_bits, group_bits)
        row_cos[s] = turn_cos(here)
        row_sin[s] = turn_sin(here)

    def stem(c):
        b_copies[c].wait()
        rights = []
        for j in range(slices):
            b_real = b_vm[c, 0, j]
            b_imag = b_vm[c, 1, j]
            rights.append(jnp.concatenate((b_real, b_imag), 1))
            rights.append(jnp.concatenate((-b_imag, b_real), 1))
        reals, imags = [], []
        for s in range(group):
            total = None
            for j in range(slices):
                for part in range(2):
                    term = jnp.dot(
                        a_vm[part, j, pl.ds(s * rows_loc, rows_loc), :],
                        rights[2 * j + part],
                        preferred_element_type=f32,
                    )
                    total = term if total is None else total + term
            real, imag = total[:, :width], total[:, width:]
            cos, sin = row_cos[s], row_sin[s]
            reals.append(real * cos - imag * sin)
            imags.append(real * sin + imag * cos)
        reals = butterfly(reals)
        imags = butterfly(imags)
        for s in range(group):
            slc, sub = s // n_sub, s % n_sub
            sub_out[c, sub, slc, :, :width] = reals[s]
            sub_out[c, sub, slc, :, width:] = imags[s]

    def sub_copies(c):
        copies = []
        for k in range(1, n_sub):
            peer = lax.rem(me_sub + k, n_sub)
            copies.append(
                pltpu.make_async_remote_copy(
                    src_ref=sub_out.at[c, peer], dst_ref=sub_in.at[c, k - 1],
                    send_sem=sub_ss.at[c, k - 1], recv_sem=sub_rs.at[c, k - 1],
                    device_id={"sub": peer}, device_id_type=MESH,
                )
            )
        return copies

    def slc_copies(c):
        copies = []
        for k in range(1, n_slc):
            peer = lax.rem(me_slc + k, n_slc)
            copies.append(
                pltpu.make_async_remote_copy(
                    src_ref=slc_out.at[c, k - 1], dst_ref=slc_in.at[c, k - 1],
                    send_sem=slc_ss.at[c, k - 1], recv_sem=slc_rs.at[c, k - 1],
                    device_id={"slc": peer}, device_id_type=MESH,
                )
            )
        return copies

    def wide_copies(c):
        copies = []
        for k in range(1, n_wide):
            peer = lax.rem(me_wide + k, n_wide)
            copies.append(
                pltpu.make_async_remote_copy(
                    src_ref=wide_out.at[c, peer, pl.ds(0, loc)],
                    dst_ref=wide_in.at[c, k - 1, pl.ds(0, loc)],
                    send_sem=wide_ss.at[c, k - 1], recv_sem=wide_rs.at[c, k - 1],
                    device_id={"wide": peer}, device_id_type=MESH,
                )
            )
        return copies

    all_sub = [sub_copies(c) for c in range(chunks)]
    all_slc = [slc_copies(c) for c in range(chunks)]
    all_wide = [wide_copies(c) for c in range(chunks)]

    def to_slc(c):
        for copy in all_sub[c]:
            copy.wait_recv()
        for k in range(1, n_slc):
            peer = lax.rem(me_slc + k, n_slc)
            total = sub_out[c, me_sub, peer]
            for j in range(n_sub - 1):
                total = total + sub_in[c, j, peer]
            slc_out[c, k - 1] = total
            all_slc[c][k - 1].start()

    col_turns = vector_turns(lax.broadcasted_iota(i32, (1, columns), 1), row_bits, col_bits)
    col_cos = turn_cos(col_turns)
    col_sin = turn_sin(col_turns)

    def to_wide(c):
        total = sub_out[c, me_sub, me_slc]
        for j in range(n_sub - 1):
            total = total + sub_in[c, j, me_slc]
        for k in range(1, n_slc):
            all_slc[c][k - 1].wait_recv()
            total = total + slc_in[c, k - 1]
        real, imag = total[:, :width], total[:, width:]
        cos = col_cos[:, c * width:(c + 1) * width]
        sin = col_sin[:, c * width:(c + 1) * width]
        turned = jnp.concatenate((real * cos - imag * sin, real * sin + imag * cos), 1)
        top, rest = split_two(turned)
        mat = row_mat[...]
        mixed = jnp.dot(mat, top, preferred_element_type=f32) + jnp.dot(
            mat, rest, preferred_element_type=f32
        )
        for h in range(n_wide):
            wide_out[c, h] = mixed[h * loc_pad:(h + 1) * loc_pad]
        for copy in all_wide[c]:
            copy.start()

    def finish(c):
        for copy in all_wide[c]:
            copy.wait_recv()
        wide_in[c, n_wide - 1] = wide_out[c, me_wide]
        blocks = []
        for w in range(n_wide):
            slot = lax.rem(me_wide - w - 1 + 2 * n_wide, n_wide)
            blocks.append(wide_in[c, slot])
        blocks = butterfly(blocks)
        stacked = jnp.concatenate(
            [b[:, :width] for b in blocks] + [b[:, width:] for b in blocks], 0
        )
        top, rest = split_two(stacked)
        mat = col_mat[pl.ds(c * width, width), :]
        term = jnp.dot(top, mat, preferred_element_type=f32) + jnp.dot(
            rest, mat, preferred_element_type=f32
        )
        if c == 0:
            acc[...] = term
        elif c < chunks - 1:
            acc[...] += term
        else:
            total = acc[...] + term
            half = n_wide * loc_pad
            real, imag = total[:half], total[half:]
            cos, sin = out_cos[...], out_sin[...]
            out_real = real * cos + imag * sin
            out_imag = imag * cos - real * sin
            for w in range(n_wide):
                out_ref[0, w] = out_real[w * loc_pad:w * loc_pad + loc]
                out_ref[1, w] = out_imag[w * loc_pad:w * loc_pad + loc]

    a_copy.wait()
    stem(0)
    pl.semaphore_wait(barrier, (n_sub - 1) + (n_slc - 1) + (n_wide - 1))
    for copy in all_sub[0]:
        copy.start()
    for c in range(1, chunks):
        stem(c)
        for copy in all_sub[c]:
            copy.start()
        to_slc(c - 1)
    to_slc(chunks - 1)

    shape = (n_wide * loc_pad, rows_loc)
    spot = lax.broadcasted_iota(i32, shape, 0)
    low = spot & (loc_pad - 1)
    high = lax.shift_right_logical(spot, jnp.full_like(spot, loc_pad.bit_length() - 1))
    entry = sign_of(high * loc + low, lax.broadcasted_iota(i32, shape, 1))
    row_mat[...] = jnp.where(low < loc, entry, 0.0).astype(jnp.bfloat16)

    positions = lax.broadcasted_iota(i32, (1, columns), 1)
    source = jnp.zeros((1, columns), i32)
    for j in range(col_bits):
        source = source + bit_of(positions, j) * lax.shift_left(jnp.int32(1), order_ref[j])
    for c in range(chunks):
        inner = lax.broadcasted_iota(i32, (width, columns), 0) + c * width
        col_mat[pl.ds(c * width, width), :] = sign_of(
            jnp.broadcast_to(source, (width, columns)), inner
        ).astype(jnp.bfloat16)

    legs = row_bits + col_bits
    scale = 0.5 ** (legs // 2) * (HALF_ROOT if legs % 2 else 1.0)
    place = lax.broadcasted_iota(i32, (n_wide * loc_pad, 1), 0)
    inner_loc = place & (loc_pad - 1)
    outer = lax.shift_right_logical(place, jnp.full_like(place, loc_pad.bit_length() - 1))
    end_turns = vector_turns(outer, 0, wide_bits)
    end_turns = end_turns + vector_turns(inner_loc, row_bits - loc_bits, loc_bits)
    end_turns = end_turns + scalar_turns(me_group.astype(i32), wide_bits, group_bits)
    end_turns = end_turns + scalar_turns(me_wide.astype(i32), wide_bits + group_bits, rows_bits - loc_bits)
    end_turns = end_turns + vector_turns(source, row_bits, col_bits)
    out_cos[...] = turn_cos(end_turns) * scale
    out_sin[...] = turn_sin(end_turns) * scale

    to_wide(0)
    for c in range(1, chunks):
        to_wide(c)
        finish(c - 1)
    finish(chunks - 1)
    for copies in all_sub + all_slc + all_wide:
        for copy in copies:
            copy.wait_send()


def per_device(a_stem, b_stem, gate_pick, leg_order):
    columns = b_stem.shape[3]
    slices = a_stem.shape[1]
    bond = a_stem.shape[3]
    n_wide = lax.axis_size("wide")
    n_slc = lax.axis_size("slc")
    n_sub = lax.axis_size("sub")
    group = n_slc * n_sub
    rows_dev = a_stem.shape[2]
    rows_loc = rows_dev // group
    loc = rows_loc // n_wide
    loc_pad = max(loc, 8)
    width = 128
    chunks = columns // width
    dims = (n_sub, n_slc, n_wide, slices, rows_loc, loc, loc_pad, columns, width)
    f32, bf16 = jnp.float32, jnp.bfloat16
    tall = n_wide * loc_pad
    dma = pltpu.SemaphoreType.DMA
    out = pl.pallas_call(
        functools.partial(kernel_body, dims),
        out_shape=jax.ShapeDtypeStruct((2, n_wide, loc, columns), f32),
        in_specs=[
            pl.BlockSpec(memory_space=pltpu.SMEM),
            pl.BlockSpec(memory_space=pltpu.SMEM),
            pl.BlockSpec(memory_space=pl.ANY),
            pl.BlockSpec(memory_space=pl.ANY),
        ],
        out_specs=pl.BlockSpec(memory_space=pltpu.VMEM),
        scratch_shapes=[
            pltpu.VMEM((2, slices, rows_dev, bond), bf16),
            pltpu.VMEM((chunks, 2, slices, bond, width), bf16),
            pltpu.VMEM((group, rows_loc, 128), f32),
            pltpu.VMEM((group, rows_loc, 128), f32),
            pltpu.VMEM((tall, rows_loc), bf16),
            pltpu.VMEM((columns, columns), bf16),
            pltpu.VMEM((tall, columns), f32),
            pltpu.VMEM((tall, columns), f32),
            pltpu.VMEM((chunks, n_sub, n_slc, rows_loc, 2 * width), f32),
            pltpu.VMEM((chunks, n_sub - 1, n_slc, rows_loc, 2 * width), f32),
            pltpu.VMEM((chunks, n_slc - 1, rows_loc, 2 * width), f32),
            pltpu.VMEM((chunks, n_slc - 1, rows_loc, 2 * width), f32),
            pltpu.VMEM((chunks, n_wide, loc_pad, 2 * width), f32),
            pltpu.VMEM((chunks, n_wide, loc_pad, 2 * width), f32),
            pltpu.VMEM((2 * tall, columns), f32),
            dma,
            dma((chunks,)),
            dma((chunks, n_sub - 1)),
            dma((chunks, n_sub - 1)),
            dma((chunks, n_slc - 1)),
            dma((chunks, n_slc - 1)),
            dma((chunks, n_wide - 1)),
            dma((chunks, n_wide - 1)),
        ],
        compiler_params=pltpu.CompilerParams(
            collective_id=0, has_side_effects=True, vmem_limit_bytes=48 * 2**20
        ),
    )(gate_pick, leg_order, a_stem, b_stem)
    return out.reshape(2, n_wide, 1, 1, loc, columns)


def solution(mesh):
    placed = (
        P(None, ("grp", "slc", "sub"), "wide", None),
        P(None, ("grp", "slc", "sub"), None, None),
        P("grp"),
        P("grp"),
    )
    return jax.shard_map(
        per_device,
        mesh=mesh,
        in_specs=placed,
        out_specs=P(None, "grp", ("slc", "sub"), "wide", None, None),
        check_vma=False,
    )
```

```python
import functools

import jax
import jax.numpy as jnp
from jax import lax
from jax.experimental import pallas as pl
from jax.experimental.pallas import tpu as pltpu
from jax.sharding import PartitionSpec as P

HALF_ROOT = 0.7071067811865476
MESH = pl.DeviceIdType.MESH


def eighth_turns(pick):
    return jnp.where(pick == 0, 2, jnp.where(pick == 2, 1, 0)).astype(jnp.int32)


def bit_of(value, position):
    return lax.shift_right_logical(value, jnp.full_like(value, position)) & 1


def turn_cos(turns):
    angle = turns & 7
    size = jnp.where((angle & 1) == 1, HALF_ROOT, jnp.where((angle & 2) == 0, 1.0, 0.0))
    return jnp.where(((angle + 2) & 4) == 4, -size, size).astype(jnp.float32)


def turn_sin(turns):
    return turn_cos(turns + 6)


def sign_of(target, source):
    value = (~target) & source
    for step in (8, 4, 2, 1):
        value = value ^ lax.shift_right_logical(value, jnp.full_like(value, step))
    return (1 - 2 * (value & 1)).astype(jnp.float32)


def butterfly(blocks):
    count = len(blocks)
    mask = 1
    while mask < count:
        mixed = list(blocks)
        for index in range(count):
            if not index & mask:
                low, high = blocks[index], blocks[index | mask]
                mixed[index] = low - high
                mixed[index | mask] = low + high
        blocks = mixed
        mask *= 2
    return blocks


def split_two(value):
    top = value.astype(jnp.bfloat16)
    rest = (value - top.astype(jnp.float32)).astype(jnp.bfloat16)
    return top, rest


def kernel_body(
    dims,
    pick_hbm, order_hbm, a_hbm, b_hbm, out_ref,
    pick_ref, order_ref, a_vm, b_vm, row_cos, row_sin, row_mat, col_mat, out_cos, out_sin,
    sub_out, sub_in, slc_out, slc_in, wide_out, wide_in, acc,
    pick_sem, order_sem, a_sem, b_sem, sub_ss, sub_rs, slc_ss, slc_rs, wide_ss, wide_rs,
    lower_in, upper_in,
):
    (n_sub, n_slc, n_wide, slices, rows_loc, loc, loc_pad, columns, width) = dims
    f32 = jnp.float32
    i32 = jnp.int32
    group = n_sub * n_slc
    chunks = columns // width
    col_bits = columns.bit_length() - 1
    wide_bits = n_wide.bit_length() - 1
    group_bits = group.bit_length() - 1
    rows_bits = rows_loc.bit_length() - 1
    loc_bits = loc.bit_length() - 1
    row_bits = wide_bits + group_bits + rows_bits
    me_sub = lax.axis_index("sub")
    me_slc = lax.axis_index("slc")
    me_wide = lax.axis_index("wide")
    me_group = me_slc * n_sub + me_sub

    barrier = pltpu.get_barrier_semaphore()
    for axis, me, count in (("sub", me_sub, n_sub), ("slc", me_slc, n_slc)):
        for k in range(1, count):
            pl.semaphore_signal(
                barrier, inc=1, device_id={axis: lax.rem(me + k, count)}, device_id_type=MESH
            )

    @pl.when(me_wide > 0)
    def _():
        pl.semaphore_signal(barrier, inc=1, device_id={"wide": me_wide - 1}, device_id_type=MESH)

    @pl.when(me_wide < n_wide - 1)
    def _():
        pl.semaphore_signal(barrier, inc=1, device_id={"wide": me_wide + 1}, device_id_type=MESH)

    pick_copy = pltpu.make_async_copy(pick_hbm, pick_ref, pick_sem)
    order_copy = pltpu.make_async_copy(order_hbm, order_ref, order_sem)
    a_copy = pltpu.make_async_copy(a_hbm, a_vm, a_sem)
    b_copies = [
        pltpu.make_async_copy(
            b_hbm.at[:, :, :, pl.ds(c * width, width)], b_vm.at[c], b_sem.at[c]
        )
        for c in range(chunks)
    ]
    pick_copy.start()
    order_copy.start()
    b_copies[0].start()
    a_copy.start()
    for c in range(1, chunks):
        b_copies[c].start()

    shape = (n_wide * loc_pad, rows_loc)
    spot = lax.broadcasted_iota(i32, shape, 0)
    low = spot & (loc_pad - 1)
    high = lax.shift_right_logical(spot, jnp.full_like(spot, loc_pad.bit_length() - 1))
    entry = sign_of(high * loc + low, lax.broadcasted_iota(i32, shape, 1))
    row_mat[...] = jnp.where(low < loc, entry, 0.0).astype(jnp.bfloat16)

    pick_copy.wait()
    order_copy.wait()
    turns = [eighth_turns(pick_ref[q]) for q in range(row_bits + col_bits)]

    def scalar_turns(value, first, count):
        total = jnp.int32(0)
        for j in range(count):
            total = total + turns[first + count - 1 - j] * (lax.shift_right_logical(value, jnp.int32(j)) & 1)
        return total

    def vector_turns(value, first, count):
        total = jnp.zeros_like(value)
        for j in range(count):
            total = total + turns[first + count - 1 - j] * bit_of(value, j)
        return total

    row_iota = lax.broadcasted_iota(i32, (rows_loc, 128), 0)
    row_turns = vector_turns(row_iota, wide_bits + group_bits, rows_bits)
    row_turns = row_turns + scalar_turns(me_wide.astype(i32), 0, wide_bits)
    for s in range(group):
        here = row_turns + scalar_turns(jnp.int32(s), wide_bits, group_bits)
        row_cos[s] = turn_cos(here)
        row_sin[s] = turn_sin(here)
    col_turns = vector_turns(lax.broadcasted_iota(i32, (1, columns), 1), row_bits, col_bits)
    col_cos = turn_cos(col_turns)
    col_sin = turn_sin(col_turns)

    def stem(c):
        b_copies[c].wait()
        rights = []
        for j in range(slices):
            b_real = b_vm[c, 0, j]
            b_imag = b_vm[c, 1, j]
            rights.append(jnp.concatenate((b_real, b_imag), 1))
            rights.append(jnp.concatenate((-b_imag, b_real), 1))
        right = jnp.concatenate(rights, 0)
        ccos = col_cos[:, c * width:(c + 1) * width]
        csin = col_sin[:, c * width:(c + 1) * width]
        reals, imags = [], []
        for s in range(group):
            left = jnp.concatenate(
                [
                    a_vm[part, j, pl.ds(s * rows_loc, rows_loc), :]
                    for j in range(slices)
                    for part in range(2)
                ],
                1,
            )
            total = jnp.dot(left, right, preferred_element_type=f32)
            real, imag = total[:, :width], total[:, width:]
            cos, sin = row_cos[s], row_sin[s]
            real, imag = real * cos - imag * sin, real * sin + imag * cos
            reals.append(real * ccos - imag * csin)
            imags.append(real * csin + imag * ccos)
        reals = butterfly(reals)
        imags = butterfly(imags)
        mat = row_mat[...]
        for s in range(group):
            slc, sub = s // n_sub, s % n_sub
            top, rest = split_two(jnp.concatenate((reals[s], imags[s]), 1))
            mixed = jnp.dot(mat, top, preferred_element_type=f32) + jnp.dot(
                mat, rest, preferred_element_type=f32
            )
            for h in range(n_wide):
                sub_out[c, sub, slc, h] = mixed[h * loc_pad:(h + 1) * loc_pad]

    def place_of(i):
        left = jnp.where(i < n_wide - 1 - me_wide, n_wide - 1 - i, i - (n_wide - 1 - me_wide))
        right = jnp.where(i < me_wide, i, n_wide - 1 - (i - me_wide))
        return jnp.where(me_wide < n_wide // 2, left, right)

    places = [place_of(i) for i in range(n_wide - 1)] + [me_wide]

    all_sub = []
    for c in range(chunks):
        for k in range(1, n_sub):
            peer = lax.rem(me_sub + k, n_sub)
            all_sub.append(
                pltpu.make_async_remote_copy(
                    src_ref=sub_out.at[c, peer], dst_ref=sub_in.at[c, k - 1],
                    send_sem=sub_ss.at[c, k - 1], recv_sem=sub_rs.at[c, k - 1],
                    device_id={"sub": peer}, device_id_type=MESH,
                )
            )

    def slc_copy(i, c, k):
        return pltpu.make_async_remote_copy(
            src_ref=slc_out.at[i, c, k - 1], dst_ref=slc_in.at[i, c, k - 1],
            send_sem=slc_ss.at[i, c, k - 1], recv_sem=slc_rs.at[i, c, k - 1],
            device_id={"slc": lax.rem(me_slc + k, n_slc)}, device_id_type=MESH,
        )

    all_slc = {
        (i, c, k): slc_copy(i, c, k)
        for i in range(n_wide) for c in range(chunks) for k in range(1, n_slc)
    }

    def wide_copy(i, c, owner):
        return pltpu.make_async_remote_copy(
            src_ref=wide_out.at[i, c, pl.ds(0, loc)],
            dst_ref=wide_in.at[owner, c, pl.ds(0, loc)],
            send_sem=wide_ss.at[i, c], recv_sem=wide_rs.at[owner, c],
            device_id={"wide": places[i]}, device_id_type=MESH,
        )

    all_wide = {
        (i, c): wide_copy(i, c, me_wide) for i in range(n_wide - 1) for c in range(chunks)
    }

    def send_sub(c):
        for k in range(n_sub - 1):
            all_sub[c * (n_sub - 1) + k].start()

    def to_slc(i, c):
        if i == 0:
            for k in range(n_sub - 1):
                all_sub[c * (n_sub - 1) + k].wait_recv()
        for k in range(1, n_slc):
            peer = lax.rem(me_slc + k, n_slc)
            total = sub_out[c, me_sub, peer, places[i]]
            for j in range(n_sub - 1):
                total = total + sub_in[c, j, peer, places[i]]
            slc_out[i, c, k - 1] = total
            all_slc[i, c, k].start()

    def summed(i, c):
        total = sub_out[c, me_sub, me_slc, places[i]]
        for j in range(n_sub - 1):
            total = total + sub_in[c, j, me_slc, places[i]]
        for k in range(1, n_slc):
            all_slc[i, c, k].wait_recv()
            total = total + slc_in[i, c, k - 1]
        return total

    def to_wide(i, c):
        wide_out[i, c] = summed(i, c)
        all_wide[i, c].start()

    def finish(i):
        pieces = []
        for c in range(chunks):
            if i < n_wide - 1:
                wide_copy(i, c, places[i]).wait_recv()
                pieces.append(wide_in[places[i], c])
            else:
                pieces.append(summed(i, c))
        stacked = jnp.concatenate(
            (
                jnp.concatenate([piece[:, :width] for piece in pieces], 1),
                jnp.concatenate([piece[:, width:] for piece in pieces], 1),
            ),
            0,
        )
        top, rest = split_two(stacked)
        both = jnp.dot(
            jnp.concatenate((top, rest), 0), col_mat[...], preferred_element_type=f32
        )
        acc[places[i]] = both[:2 * loc_pad] + both[2 * loc_pad:]

    a_copy.wait()
    ahead = min(3, chunks)
    for c in range(ahead):
        stem(c)
    ends = jnp.where(me_wide == 0, 1, 0) + jnp.where(me_wide == n_wide - 1, 1, 0)
    pl.semaphore_wait(barrier, (n_sub - 1) + (n_slc - 1) + 2 - ends)
    for c in range(ahead):
        send_sub(c)

    def tell(token, target):
        pl.semaphore_signal(token, inc=1, device_id={"wide": target}, device_id_type=MESH)

    if n_wide > 2:
        @pl.when(me_wide == n_wide - 2)
        def _():
            tell(upper_in, me_wide - 1)

        @pl.when(me_wide == 1)
        def _():
            tell(lower_in, me_wide + 1)

    for c in range(ahead, chunks):
        stem(c)
        send_sub(c)
    for c in range(chunks):
        to_slc(0, c)

    if n_wide > 2:
        @pl.when(me_wide <= n_wide - 3)
        def _():
            pl.semaphore_wait(upper_in, 1)

            @pl.when(me_wide >= 1)
            def _():
                tell(upper_in, me_wide - 1)

        @pl.when(me_wide >= 2)
        def _():
            pl.semaphore_wait(lower_in, 1)

            @pl.when(me_wide <= n_wide - 2)
            def _():
                tell(lower_in, me_wide + 1)

    for i in range(1, n_wide):
        for c in range(chunks):
            to_slc(i, c)

    positions = lax.broadcasted_iota(i32, (1, columns), 1)
    source = jnp.zeros((1, columns), i32)
    for j in range(col_bits):
        source = source + bit_of(positions, j) * lax.shift_left(jnp.int32(1), order_ref[j])

    def build_columns(c):
        inner = lax.broadcasted_iota(i32, (width, columns), 0) + c * width
        col_mat[pl.ds(c * width, width), :] = sign_of(
            jnp.broadcast_to(source, (width, columns)), inner
        ).astype(jnp.bfloat16)

    def build_exit():
        legs = row_bits + col_bits
        scale = 0.5 ** (legs // 2) * (HALF_ROOT if legs % 2 else 1.0)
        place = lax.broadcasted_iota(i32, (n_wide * loc_pad, 1), 0)
        inner_loc = place & (loc_pad - 1)
        outer = lax.shift_right_logical(place, jnp.full_like(place, loc_pad.bit_length() - 1))
        end = vector_turns(outer, 0, wide_bits)
        end = end + vector_turns(inner_loc, row_bits - loc_bits, loc_bits)
        end = end + scalar_turns(me_group.astype(i32), wide_bits, group_bits)
        end = end + scalar_turns(me_wide.astype(i32), wide_bits + group_bits, rows_bits - loc_bits)
        end = end + vector_turns(source, row_bits, col_bits)
        out_cos[...] = turn_cos(end) * scale
        out_sin[...] = turn_sin(end) * scale

    for c in range(chunks):
        build_columns(c)
    for i in range(n_wide - 1):
        for c in range(chunks):
            to_wide(i, c)
    build_exit()
    for i in range(n_wide - 2):
        finish(i)
    finish(n_wide - 1)
    finish(n_wide - 2)
    blocks = butterfly([acc[w] for w in range(n_wide)])
    for w in range(n_wide):
        real, imag = blocks[w][:loc], blocks[w][loc_pad:loc_pad + loc]
        cos = out_cos[w * loc_pad:w * loc_pad + loc]
        sin = out_sin[w * loc_pad:w * loc_pad + loc]
        out_ref[0, w] = real * cos + imag * sin
        out_ref[1, w] = imag * cos - real * sin
    for copy in all_sub + list(all_slc.values()) + list(all_wide.values()):
        copy.wait_send()


def per_device(a_stem, b_stem, gate_pick, leg_order):
    columns = b_stem.shape[3]
    slices = a_stem.shape[1]
    bond = a_stem.shape[3]
    n_wide = lax.axis_size("wide")
    n_slc = lax.axis_size("slc")
    n_sub = lax.axis_size("sub")
    group = n_slc * n_sub
    rows_dev = a_stem.shape[2]
    rows_loc = rows_dev // group
    loc = rows_loc // n_wide
    loc_pad = max(loc, 8)
    width = 128
    chunks = columns // width
    dims = (n_sub, n_slc, n_wide, slices, rows_loc, loc, loc_pad, columns, width)
    f32, bf16 = jnp.float32, jnp.bfloat16
    tall = n_wide * loc_pad
    dma = pltpu.SemaphoreType.DMA
    block = (loc_pad, 2 * width)
    out = pl.pallas_call(
        functools.partial(kernel_body, dims),
        out_shape=jax.ShapeDtypeStruct((2, n_wide, loc, columns), f32),
        in_specs=[pl.BlockSpec(memory_space=pltpu.HBM)] * 4,
        out_specs=pl.BlockSpec(memory_space=pltpu.VMEM),
        scratch_shapes=[
            pltpu.SMEM(gate_pick.shape, jnp.int32),
            pltpu.SMEM(leg_order.shape, jnp.int32),
            pltpu.VMEM((2, slices, rows_dev, bond), bf16),
            pltpu.VMEM((chunks, 2, slices, bond, width), bf16),
            pltpu.VMEM((group, rows_loc, 128), f32),
            pltpu.VMEM((group, rows_loc, 128), f32),
            pltpu.VMEM((tall, rows_loc), bf16),
            pltpu.VMEM((columns, columns), bf16),
            pltpu.VMEM((tall, columns), f32),
            pltpu.VMEM((tall, columns), f32),
            pltpu.VMEM((chunks, n_sub, n_slc, n_wide) + block, f32),
            pltpu.VMEM((chunks, n_sub - 1, n_slc, n_wide) + block, f32),
            pltpu.VMEM((n_wide, chunks, n_slc - 1) + block, f32),
            pltpu.VMEM((n_wide, chunks, n_slc - 1) + block, f32),
            pltpu.VMEM((n_wide, chunks) + block, f32),
            pltpu.VMEM((n_wide, chunks) + block, f32),
            pltpu.VMEM((n_wide, 2 * loc_pad, columns), f32),
            dma,
            dma,
            dma,
            dma((chunks,)),
            dma((chunks, n_sub - 1)),
            dma((chunks, n_sub - 1)),
            dma((n_wide, chunks, n_slc - 1)),
            dma((n_wide, chunks, n_slc - 1)),
            dma((n_wide, chunks)),
            dma((n_wide, chunks)),
            pltpu.SemaphoreType.REGULAR,
            pltpu.SemaphoreType.REGULAR,
        ],
        compiler_params=pltpu.CompilerParams(
            collective_id=0, has_side_effects=True, vmem_limit_bytes=48 * 2**20
        ),
    )(gate_pick, leg_order, a_stem, b_stem)
    return out.reshape(2, n_wide, 1, 1, loc, columns)


def solution(mesh):
    placed = (
        P(None, ("grp", "slc", "sub"), "wide", None),
        P(None, ("grp", "slc", "sub"), None, None),
        P("grp"),
        P("grp"),
    )
    return jax.shard_map(
        per_device,
        mesh=mesh,
        in_specs=placed,
        out_specs=P(None, "grp", ("slc", "sub"), "wide", None, None),
        check_vma=False,
    )
```

```python
import functools

import jax
import jax.numpy as jnp
from jax import lax
from jax.experimental import pallas as pl
from jax.experimental.pallas import tpu as pltpu
from jax.sharding import PartitionSpec as P

HALF_ROOT = 0.7071067811865476
MESH = pl.DeviceIdType.MESH


def eighth_turns(pick):
    return jnp.where(pick == 0, 2, jnp.where(pick == 2, 1, 0)).astype(jnp.int32)


def bit_of(value, position):
    return lax.shift_right_logical(value, jnp.full_like(value, position)) & 1


def turn_cos(turns):
    angle = turns & 7
    size = jnp.where((angle & 1) == 1, HALF_ROOT, jnp.where((angle & 2) == 0, 1.0, 0.0))
    return jnp.where(((angle + 2) & 4) == 4, -size, size).astype(jnp.float32)


def turn_sin(turns):
    return turn_cos(turns + 6)


def sign_of(target, source):
    value = (~target) & source
    for step in (8, 4, 2, 1):
        value = value ^ lax.shift_right_logical(value, jnp.full_like(value, step))
    return (1 - 2 * (value & 1)).astype(jnp.float32)


def butterfly(blocks):
    count = len(blocks)
    mask = 1
    while mask < count:
        mixed = list(blocks)
        for index in range(count):
            if not index & mask:
                low, high = blocks[index], blocks[index | mask]
                mixed[index] = low - high
                mixed[index | mask] = low + high
        blocks = mixed
        mask *= 2
    return blocks


def split_two(value):
    top = value.astype(jnp.bfloat16)
    rest = (value - top.astype(jnp.float32)).astype(jnp.bfloat16)
    return top, rest


def kernel_body(
    dims,
    pick_hbm, a_hbm, b_hbm, out_ref,
    pick_ref, a_vm, b_vm, row_cos, row_sin, row_mat, col_mat, out_cos, out_sin,
    sub_out, sub_in, slc_out, slc_in, wide_out, wide_in, acc,
    pick_sem, a_sem, b_sem, sub_ss, sub_rs, slc_ss, slc_rs, wide_ss, wide_rs,
    lower_in, upper_in,
):
    (n_sub, n_slc, n_wide, slices, rows_loc, loc, loc_pad, columns, width) = dims
    f32 = jnp.float32
    i32 = jnp.int32
    group = n_sub * n_slc
    chunks = columns // width
    col_bits = columns.bit_length() - 1
    wide_bits = n_wide.bit_length() - 1
    group_bits = group.bit_length() - 1
    rows_bits = rows_loc.bit_length() - 1
    loc_bits = loc.bit_length() - 1
    row_bits = wide_bits + group_bits + rows_bits
    me_sub = lax.axis_index("sub")
    me_slc = lax.axis_index("slc")
    me_wide = lax.axis_index("wide")
    me_group = me_slc * n_sub + me_sub

    barrier = pltpu.get_barrier_semaphore()
    for axis, me, count in (("sub", me_sub, n_sub), ("slc", me_slc, n_slc)):
        for k in range(1, count):
            pl.semaphore_signal(
                barrier, inc=1, device_id={axis: lax.rem(me + k, count)}, device_id_type=MESH
            )

    @pl.when(me_wide > 0)
    def _():
        pl.semaphore_signal(barrier, inc=1, device_id={"wide": me_wide - 1}, device_id_type=MESH)

    @pl.when(me_wide < n_wide - 1)
    def _():
        pl.semaphore_signal(barrier, inc=1, device_id={"wide": me_wide + 1}, device_id_type=MESH)

    pick_copy = pltpu.make_async_copy(pick_hbm, pick_ref, pick_sem)
    a_copy = pltpu.make_async_copy(a_hbm, a_vm, a_sem)
    b_copies = [
        pltpu.make_async_copy(
            b_hbm.at[:, :, :, pl.ds(c * width, width)], b_vm.at[c], b_sem.at[c]
        )
        for c in range(chunks)
    ]
    pick_copy.start()
    b_copies[0].start()
    a_copy.start()
    for c in range(1, chunks):
        b_copies[c].start()

    shape = (n_wide * loc_pad, rows_loc)
    spot = lax.broadcasted_iota(i32, shape, 0)
    low = spot & (loc_pad - 1)
    high = lax.shift_right_logical(spot, jnp.full_like(spot, loc_pad.bit_length() - 1))
    entry = sign_of(high * loc + low, lax.broadcasted_iota(i32, shape, 1))
    row_mat[...] = jnp.where(low < loc, entry, 0.0).astype(jnp.bfloat16)

    pick_copy.wait()
    turns = [eighth_turns(pick_ref[q]) for q in range(row_bits + col_bits)]

    def scalar_turns(value, first, count):
        total = jnp.int32(0)
        for j in range(count):
            total = total + turns[first + count - 1 - j] * (lax.shift_right_logical(value, jnp.int32(j)) & 1)
        return total

    def vector_turns(value, first, count):
        total = jnp.zeros_like(value)
        for j in range(count):
            total = total + turns[first + count - 1 - j] * bit_of(value, j)
        return total

    row_iota = lax.broadcasted_iota(i32, (rows_loc, 128), 0)
    row_turns = vector_turns(row_iota, wide_bits + group_bits, rows_bits)
    row_turns = row_turns + scalar_turns(me_wide.astype(i32), 0, wide_bits)
    for s in range(group):
        here = row_turns + scalar_turns(jnp.int32(s), wide_bits, group_bits)
        row_cos[s] = turn_cos(here)
        row_sin[s] = turn_sin(here)
    col_turns = vector_turns(lax.broadcasted_iota(i32, (1, columns), 1), row_bits, col_bits)
    col_cos = turn_cos(col_turns)
    col_sin = turn_sin(col_turns)

    def stem(c):
        b_copies[c].wait()
        rights = []
        for j in range(slices):
            b_real = b_vm[c, 0, j]
            b_imag = b_vm[c, 1, j]
            rights.append(jnp.concatenate((b_real, b_imag), 1))
            rights.append(jnp.concatenate((-b_imag, b_real), 1))
        right = jnp.concatenate(rights, 0)
        ccos = col_cos[:, c * width:(c + 1) * width]
        csin = col_sin[:, c * width:(c + 1) * width]
        reals, imags = [], []
        for s in range(group):
            left = jnp.concatenate(
                [
                    a_vm[part, j, pl.ds(s * rows_loc, rows_loc), :]
                    for j in range(slices)
                    for part in range(2)
                ],
                1,
            )
            total = jnp.dot(left, right, preferred_element_type=f32)
            real, imag = total[:, :width], total[:, width:]
            cos, sin = row_cos[s], row_sin[s]
            real, imag = real * cos - imag * sin, real * sin + imag * cos
            reals.append(real * ccos - imag * csin)
            imags.append(real * csin + imag * ccos)
        reals = butterfly(reals)
        imags = butterfly(imags)
        mat = row_mat[...]
        for s in range(group):
            slc, sub = s // n_sub, s % n_sub
            top, rest = split_two(jnp.concatenate((reals[s], imags[s]), 1))
            mixed = jnp.dot(mat, top, preferred_element_type=f32) + jnp.dot(
                mat, rest, preferred_element_type=f32
            )
            for h in range(n_wide):
                sub_out[c, sub, slc, h] = mixed[h * loc_pad:(h + 1) * loc_pad]

    def place_of(i):
        left = jnp.where(i < n_wide - 1 - me_wide, n_wide - 1 - i, i - (n_wide - 1 - me_wide))
        right = jnp.where(i < me_wide, i, n_wide - 1 - (i - me_wide))
        return jnp.where(me_wide < n_wide // 2, left, right)

    places = [place_of(i) for i in range(n_wide - 1)] + [me_wide]

    all_sub = []
    for c in range(chunks):
        for k in range(1, n_sub):
            peer = lax.rem(me_sub + k, n_sub)
            all_sub.append(
                pltpu.make_async_remote_copy(
                    src_ref=sub_out.at[c, peer], dst_ref=sub_in.at[c, k - 1],
                    send_sem=sub_ss.at[c, k - 1], recv_sem=sub_rs.at[c, k - 1],
                    device_id={"sub": peer}, device_id_type=MESH,
                )
            )

    def slc_copy(i, c, k):
        return pltpu.make_async_remote_copy(
            src_ref=slc_out.at[i, c, k - 1], dst_ref=slc_in.at[i, c, k - 1],
            send_sem=slc_ss.at[i, c, k - 1], recv_sem=slc_rs.at[i, c, k - 1],
            device_id={"slc": lax.rem(me_slc + k, n_slc)}, device_id_type=MESH,
        )

    all_slc = {
        (i, c, k): slc_copy(i, c, k)
        for i in range(n_wide) for c in range(chunks) for k in range(1, n_slc)
    }

    def wide_copy(i, c, owner):
        return pltpu.make_async_remote_copy(
            src_ref=wide_out.at[i, c, pl.ds(0, loc)],
            dst_ref=wide_in.at[owner, c, pl.ds(0, loc)],
            send_sem=wide_ss.at[i, c], recv_sem=wide_rs.at[owner, c],
            device_id={"wide": places[i]}, device_id_type=MESH,
        )

    all_wide = {
        (i, c): wide_copy(i, c, me_wide) for i in range(n_wide - 1) for c in range(chunks)
    }

    def send_sub(c):
        for k in range(n_sub - 1):
            all_sub[c * (n_sub - 1) + k].start()

    def to_slc(i, c):
        if i == 0:
            for k in range(n_sub - 1):
                all_sub[c * (n_sub - 1) + k].wait_recv()
        for k in range(1, n_slc):
            peer = lax.rem(me_slc + k, n_slc)
            total = sub_out[c, me_sub, peer, places[i]]
            for j in range(n_sub - 1):
                total = total + sub_in[c, j, peer, places[i]]
            slc_out[i, c, k - 1] = total
            all_slc[i, c, k].start()

    def summed(i, c):
        total = sub_out[c, me_sub, me_slc, places[i]]
        for j in range(n_sub - 1):
            total = total + sub_in[c, j, me_slc, places[i]]
        for k in range(1, n_slc):
            all_slc[i, c, k].wait_recv()
            total = total + slc_in[i, c, k - 1]
        return total

    def to_wide(i, c):
        wide_out[i, c] = summed(i, c)
        all_wide[i, c].start()

    def finish(i):
        pieces = []
        for c in range(chunks):
            if i < n_wide - 1:
                wide_copy(i, c, places[i]).wait_recv()
                pieces.append(wide_in[places[i], c])
            else:
                pieces.append(summed(i, c))
        stacked = jnp.concatenate(
            (
                jnp.concatenate([piece[:, :width] for piece in pieces], 1),
                jnp.concatenate([piece[:, width:] for piece in pieces], 1),
            ),
            0,
        )
        top, rest = split_two(stacked)
        both = jnp.dot(
            jnp.concatenate((top, rest), 0), col_mat[...], preferred_element_type=f32
        )
        acc[places[i]] = both[:2 * loc_pad] + both[2 * loc_pad:]

    a_copy.wait()
    ahead = min(1, chunks)
    for c in range(ahead):
        stem(c)
    ends = jnp.where(me_wide == 0, 1, 0) + jnp.where(me_wide == n_wide - 1, 1, 0)
    pl.semaphore_wait(barrier, (n_sub - 1) + (n_slc - 1) + 2 - ends)
    for c in range(ahead):
        send_sub(c)

    def tell(token, target):
        pl.semaphore_signal(token, inc=1, device_id={"wide": target}, device_id_type=MESH)

    if n_wide > 2:
        @pl.when(me_wide == n_wide - 2)
        def _():
            tell(upper_in, me_wide - 1)

        @pl.when(me_wide == 1)
        def _():
            tell(lower_in, me_wide + 1)

    for c in range(ahead, chunks):
        stem(c)
        send_sub(c)
    for c in range(chunks):
        to_slc(0, c)

    if n_wide > 2:
        @pl.when(me_wide <= n_wide - 3)
        def _():
            pl.semaphore_wait(upper_in, 1)

            @pl.when(me_wide >= 1)
            def _():
                tell(upper_in, me_wide - 1)

        @pl.when(me_wide >= 2)
        def _():
            pl.semaphore_wait(lower_in, 1)

            @pl.when(me_wide <= n_wide - 2)
            def _():
                tell(lower_in, me_wide + 1)

    for i in range(1, n_wide):
        for c in range(chunks):
            to_slc(i, c)

    positions = lax.broadcasted_iota(i32, (1, columns), 1)
    source = jnp.zeros((1, columns), i32)
    for j in range(col_bits):
        source = source + bit_of(positions, j) * lax.shift_left(jnp.int32(1), pick_ref[row_bits + col_bits + j])

    def build_columns(c):
        inner = lax.broadcasted_iota(i32, (width, columns), 0) + c * width
        col_mat[pl.ds(c * width, width), :] = sign_of(
            jnp.broadcast_to(source, (width, columns)), inner
        ).astype(jnp.bfloat16)

    def build_exit():
        legs = row_bits + col_bits
        scale = 0.5 ** (legs // 2) * (HALF_ROOT if legs % 2 else 1.0)
        place = lax.broadcasted_iota(i32, (n_wide * loc_pad, 1), 0)
        inner_loc = place & (loc_pad - 1)
        outer = lax.shift_right_logical(place, jnp.full_like(place, loc_pad.bit_length() - 1))
        end = vector_turns(outer, 0, wide_bits)
        end = end + vector_turns(inner_loc, row_bits - loc_bits, loc_bits)
        end = end + scalar_turns(me_group.astype(i32), wide_bits, group_bits)
        end = end + scalar_turns(me_wide.astype(i32), wide_bits + group_bits, rows_bits - loc_bits)
        end = end + vector_turns(source, row_bits, col_bits)
        out_cos[...] = turn_cos(end) * scale
        out_sin[...] = turn_sin(end) * scale

    for c in range(chunks):
        build_columns(c)
    for i in range(n_wide - 1):
        for c in range(chunks):
            to_wide(i, c)
    build_exit()
    for i in range(n_wide - 2):
        finish(i)
    finish(n_wide - 1)
    finish(n_wide - 2)
    blocks = butterfly([acc[w] for w in range(n_wide)])
    for w in range(n_wide):
        real, imag = blocks[w][:loc], blocks[w][loc_pad:loc_pad + loc]
        cos = out_cos[w * loc_pad:w * loc_pad + loc]
        sin = out_sin[w * loc_pad:w * loc_pad + loc]
        out_ref[0, w] = real * cos + imag * sin
        out_ref[1, w] = imag * cos - real * sin
    for copy in all_sub + list(all_slc.values()) + list(all_wide.values()):
        copy.wait_send()


def per_device(a_stem, b_stem, gate_pick, leg_order):
    columns = b_stem.shape[3]
    slices = a_stem.shape[1]
    bond = a_stem.shape[3]
    n_wide = lax.axis_size("wide")
    n_slc = lax.axis_size("slc")
    n_sub = lax.axis_size("sub")
    group = n_slc * n_sub
    rows_dev = a_stem.shape[2]
    rows_loc = rows_dev // group
    loc = rows_loc // n_wide
    loc_pad = max(loc, 8)
    width = 128
    chunks = columns // width
    dims = (n_sub, n_slc, n_wide, slices, rows_loc, loc, loc_pad, columns, width)
    f32, bf16 = jnp.float32, jnp.bfloat16
    tall = n_wide * loc_pad
    dma = pltpu.SemaphoreType.DMA
    block = (loc_pad, 2 * width)
    choices = jnp.concatenate((gate_pick, leg_order))
    out = pl.pallas_call(
        functools.partial(kernel_body, dims),
        out_shape=jax.ShapeDtypeStruct((2, n_wide, loc, columns), f32),
        in_specs=[pl.BlockSpec(memory_space=pltpu.HBM)] * 3,
        out_specs=pl.BlockSpec(memory_space=pltpu.VMEM),
        scratch_shapes=[
            pltpu.SMEM(choices.shape, jnp.int32),
            pltpu.VMEM((2, slices, rows_dev, bond), bf16),
            pltpu.VMEM((chunks, 2, slices, bond, width), bf16),
            pltpu.VMEM((group, rows_loc, 128), f32),
            pltpu.VMEM((group, rows_loc, 128), f32),
            pltpu.VMEM((tall, rows_loc), bf16),
            pltpu.VMEM((columns, columns), bf16),
            pltpu.VMEM((tall, columns), f32),
            pltpu.VMEM((tall, columns), f32),
            pltpu.VMEM((chunks, n_sub, n_slc, n_wide) + block, f32),
            pltpu.VMEM((chunks, n_sub - 1, n_slc, n_wide) + block, f32),
            pltpu.VMEM((n_wide, chunks, n_slc - 1) + block, f32),
            pltpu.VMEM((n_wide, chunks, n_slc - 1) + block, f32),
            pltpu.VMEM((n_wide, chunks) + block, f32),
            pltpu.VMEM((n_wide, chunks) + block, f32),
            pltpu.VMEM((n_wide, 2 * loc_pad, columns), f32),
            dma,
            dma,
            dma((chunks,)),
            dma((chunks, n_sub - 1)),
            dma((chunks, n_sub - 1)),
            dma((n_wide, chunks, n_slc - 1)),
            dma((n_wide, chunks, n_slc - 1)),
            dma((n_wide, chunks)),
            dma((n_wide, chunks)),
            pltpu.SemaphoreType.REGULAR,
            pltpu.SemaphoreType.REGULAR,
        ],
        compiler_params=pltpu.CompilerParams(
            collective_id=0, has_side_effects=True, vmem_limit_bytes=53 * 2**20
        ),
    )(choices, a_stem, b_stem)
    return out.reshape(2, n_wide, 1, 1, loc, columns)


def solution(mesh):
    placed = (
        P(None, ("grp", "slc", "sub"), "wide", None),
        P(None, ("grp", "slc", "sub"), None, None),
        P("grp"),
        P("grp"),
    )
    return jax.shard_map(
        per_device,
        mesh=mesh,
        in_specs=placed,
        out_specs=P(None, "grp", ("slc", "sub"), "wide", None, None),
        check_vma=False,
    )
```

```python
import functools

import jax
import jax.numpy as jnp
from jax import lax
from jax.experimental import pallas as pl
from jax.experimental.pallas import tpu as pltpu
from jax.sharding import PartitionSpec as P

HALF_ROOT = 0.7071067811865476
MESH = pl.DeviceIdType.MESH


def eighth_turns(pick):
    return jnp.where(pick == 0, 2, jnp.where(pick == 2, 1, 0)).astype(jnp.int32)


def bit_of(value, position):
    return lax.shift_right_logical(value, jnp.full_like(value, position)) & 1


def turn_cos(turns):
    angle = turns & 7
    size = jnp.where((angle & 1) == 1, HALF_ROOT, jnp.where((angle & 2) == 0, 1.0, 0.0))
    return jnp.where(((angle + 2) & 4) == 4, -size, size).astype(jnp.float32)


def turn_sin(turns):
    return turn_cos(turns + 6)


def sign_of(target, source):
    value = (~target) & source
    for step in (8, 4, 2, 1):
        value = value ^ lax.shift_right_logical(value, jnp.full_like(value, step))
    return (1 - 2 * (value & 1)).astype(jnp.float32)


def butterfly(blocks):
    count = len(blocks)
    mask = 1
    while mask < count:
        mixed = list(blocks)
        for index in range(count):
            if not index & mask:
                low, high = blocks[index], blocks[index | mask]
                mixed[index] = low - high
                mixed[index | mask] = low + high
        blocks = mixed
        mask *= 2
    return blocks


def split_two(value):
    top = value.astype(jnp.bfloat16)
    rest = (value - top.astype(jnp.float32)).astype(jnp.bfloat16)
    return top, rest


def kernel_body(
    dims,
    pick_hbm, a_hbm, b_hbm, out_ref,
    pick_ref, a_vm, b_vm, row_cos, row_sin, row_mat, col_mat, out_cos, out_sin,
    sub_out, sub_in, slc_out, slc_in, wide_out, wide_in, acc,
    pick_sem, a_sem, b_sem, sub_ss, sub_rs, slc_ss, slc_rs, wide_ss, wide_rs,
    lower_in, upper_in,
):
    (n_sub, n_slc, n_wide, slices, rows_loc, loc, loc_pad, columns, width) = dims
    f32 = jnp.float32
    i32 = jnp.int32
    group = n_sub * n_slc
    chunks = columns // width
    col_bits = columns.bit_length() - 1
    wide_bits = n_wide.bit_length() - 1
    group_bits = group.bit_length() - 1
    rows_bits = rows_loc.bit_length() - 1
    loc_bits = loc.bit_length() - 1
    row_bits = wide_bits + group_bits + rows_bits
    me_sub = lax.axis_index("sub")
    me_slc = lax.axis_index("slc")
    me_wide = lax.axis_index("wide")
    me_group = me_slc * n_sub + me_sub

    barrier = pltpu.get_barrier_semaphore()
    for axis, me, count in (("sub", me_sub, n_sub), ("slc", me_slc, n_slc)):
        for k in range(1, count):
            pl.semaphore_signal(
                barrier, inc=1, device_id={axis: lax.rem(me + k, count)}, device_id_type=MESH
            )

    @pl.when(me_wide > 0)
    def _():
        pl.semaphore_signal(barrier, inc=1, device_id={"wide": me_wide - 1}, device_id_type=MESH)

    @pl.when(me_wide < n_wide - 1)
    def _():
        pl.semaphore_signal(barrier, inc=1, device_id={"wide": me_wide + 1}, device_id_type=MESH)

    pick_copy = pltpu.make_async_copy(pick_hbm, pick_ref, pick_sem)
    a_copy = pltpu.make_async_copy(a_hbm, a_vm, a_sem)
    b_copies = [
        pltpu.make_async_copy(
            b_hbm.at[:, :, :, pl.ds(c * width, width)], b_vm.at[c], b_sem.at[c]
        )
        for c in range(chunks)
    ]
    pick_copy.start()
    b_copies[0].start()
    a_copy.start()
    for c in range(1, chunks):
        b_copies[c].start()

    shape = (n_wide * loc_pad, rows_loc)
    spot = lax.broadcasted_iota(i32, shape, 0)
    low = spot & (loc_pad - 1)
    high = lax.shift_right_logical(spot, jnp.full_like(spot, loc_pad.bit_length() - 1))
    entry = sign_of(high * loc + low, lax.broadcasted_iota(i32, shape, 1))
    entry = jnp.where(low < loc, entry, 0.0).astype(jnp.bfloat16)
    row_mat[...] = jnp.concatenate((entry, entry), 1)

    pick_copy.wait()
    turns = [eighth_turns(pick_ref[q]) for q in range(row_bits + col_bits)]

    def scalar_turns(value, first, count):
        total = jnp.int32(0)
        for j in range(count):
            total = total + turns[first + count - 1 - j] * (lax.shift_right_logical(value, jnp.int32(j)) & 1)
        return total

    def vector_turns(value, first, count):
        total = jnp.zeros_like(value)
        for j in range(count):
            total = total + turns[first + count - 1 - j] * bit_of(value, j)
        return total

    row_iota = lax.broadcasted_iota(i32, (rows_loc, 128), 0)
    row_turns = vector_turns(row_iota, wide_bits + group_bits, rows_bits)
    row_turns = row_turns + scalar_turns(me_wide.astype(i32), 0, wide_bits)
    for s in range(group):
        here = row_turns + scalar_turns(jnp.int32(s), wide_bits, group_bits)
        row_cos[s] = turn_cos(here)
        row_sin[s] = turn_sin(here)
    col_turns = vector_turns(lax.broadcasted_iota(i32, (1, columns), 1), row_bits, col_bits)
    col_cos = turn_cos(col_turns)
    col_sin = turn_sin(col_turns)

    def stem(c):
        b_copies[c].wait()
        rights = []
        for j in range(slices):
            b_real = b_vm[c, 0, j]
            b_imag = b_vm[c, 1, j]
            rights.append(jnp.concatenate((b_real, b_imag), 1))
            rights.append(jnp.concatenate((-b_imag, b_real), 1))
        right = jnp.concatenate(rights, 0)
        ccos = col_cos[:, c * width:(c + 1) * width]
        csin = col_sin[:, c * width:(c + 1) * width]
        reals, imags = [], []
        for s in range(group):
            left = jnp.concatenate(
                [
                    a_vm[part, j, pl.ds(s * rows_loc, rows_loc), :]
                    for j in range(slices)
                    for part in range(2)
                ],
                1,
            )
            total = jnp.dot(left, right, preferred_element_type=f32)
            real, imag = total[:, :width], total[:, width:]
            cos, sin = row_cos[s], row_sin[s]
            real, imag = real * cos - imag * sin, real * sin + imag * cos
            reals.append(real * ccos - imag * csin)
            imags.append(real * csin + imag * ccos)
        reals = butterfly(reals)
        imags = butterfly(imags)
        mat = row_mat[...]
        for s in range(group):
            slc, sub = s // n_sub, s % n_sub
            top, rest = split_two(jnp.concatenate((reals[s], imags[s]), 1))
            mixed = jnp.dot(
                mat, jnp.concatenate((top, rest), 0), preferred_element_type=f32
            )
            for h in range(n_wide):
                sub_out[c, sub, slc, h] = mixed[h * loc_pad:(h + 1) * loc_pad]

    def place_of(i):
        left = jnp.where(i < n_wide - 1 - me_wide, n_wide - 1 - i, i - (n_wide - 1 - me_wide))
        right = jnp.where(i < me_wide, i, n_wide - 1 - (i - me_wide))
        return jnp.where(me_wide < n_wide // 2, left, right)

    places = [place_of(i) for i in range(n_wide - 1)] + [me_wide]

    def sub_copy(c, k, turn):
        peer = lax.rem(me_sub + k, n_sub)
        row = lax.rem(me_slc + turn, n_slc)
        return pltpu.make_async_remote_copy(
            src_ref=sub_out.at[c, peer, row], dst_ref=sub_in.at[c, k - 1, row],
            send_sem=sub_ss.at[c, k - 1, turn], recv_sem=sub_rs.at[c, k - 1, turn],
            device_id={"sub": peer}, device_id_type=MESH,
        )

    all_sub = {
        (c, k, turn): sub_copy(c, k, turn)
        for c in range(chunks) for k in range(1, n_sub) for turn in range(n_slc)
    }

    def slc_copy(i, c, k):
        return pltpu.make_async_remote_copy(
            src_ref=slc_out.at[i, c, k - 1], dst_ref=slc_in.at[i, c, k - 1],
            send_sem=slc_ss.at[i, c, k - 1], recv_sem=slc_rs.at[i, c, k - 1],
            device_id={"slc": lax.rem(me_slc + k, n_slc)}, device_id_type=MESH,
        )

    all_slc = {
        (i, c, k): slc_copy(i, c, k)
        for i in range(n_wide) for c in range(chunks) for k in range(1, n_slc)
    }

    def wide_copy(i, c, owner):
        return pltpu.make_async_remote_copy(
            src_ref=wide_out.at[i, c, pl.ds(0, loc)],
            dst_ref=wide_in.at[owner, c, pl.ds(0, loc)],
            send_sem=wide_ss.at[i, c], recv_sem=wide_rs.at[owner, c],
            device_id={"wide": places[i]}, device_id_type=MESH,
        )

    all_wide = {
        (i, c): wide_copy(i, c, me_wide) for i in range(n_wide - 1) for c in range(chunks)
    }

    def send_sub(c):
        for turn in list(range(1, n_slc)) + [0]:
            for k in range(1, n_sub):
                all_sub[c, k, turn].start()

    def to_slc(i, c):
        for k in range(1, n_slc):
            if i == 0:
                for j in range(1, n_sub):
                    all_sub[c, j, k].wait_recv()
            peer = lax.rem(me_slc + k, n_slc)
            total = sub_out[c, me_sub, peer, places[i]]
            for j in range(n_sub - 1):
                total = total + sub_in[c, j, peer, places[i]]
            slc_out[i, c, k - 1] = total
            all_slc[i, c, k].start()

    def summed(i, c):
        if i == 0:
            for k in range(1, n_sub):
                all_sub[c, k, 0].wait_recv()
        total = sub_out[c, me_sub, me_slc, places[i]]
        for j in range(n_sub - 1):
            total = total + sub_in[c, j, me_slc, places[i]]
        for k in range(1, n_slc):
            all_slc[i, c, k].wait_recv()
            total = total + slc_in[i, c, k - 1]
        return total

    def to_wide(i, c):
        wide_out[i, c] = summed(i, c)
        all_wide[i, c].start()

    def finish(i):
        pieces = []
        for c in range(chunks):
            if i < n_wide - 1:
                wide_copy(i, c, places[i]).wait_recv()
                pieces.append(wide_in[places[i], c])
            else:
                pieces.append(summed(i, c))
        stacked = jnp.concatenate(
            (
                jnp.concatenate([piece[:, :width] for piece in pieces], 1),
                jnp.concatenate([piece[:, width:] for piece in pieces], 1),
            ),
            0,
        )
        top, rest = split_two(stacked)
        both = jnp.dot(
            jnp.concatenate((top, rest), 0), col_mat[...], preferred_element_type=f32
        )
        acc[places[i]] = both[:2 * loc_pad] + both[2 * loc_pad:]

    a_copy.wait()
    ahead = min(1, chunks)
    for c in range(ahead):
        stem(c)
    ends = jnp.where(me_wide == 0, 1, 0) + jnp.where(me_wide == n_wide - 1, 1, 0)
    pl.semaphore_wait(barrier, (n_sub - 1) + (n_slc - 1) + 2 - ends)
    for c in range(ahead):
        send_sub(c)

    def tell(token, target):
        pl.semaphore_signal(token, inc=1, device_id={"wide": target}, device_id_type=MESH)

    if n_wide > 2:
        @pl.when(me_wide == n_wide - 2)
        def _():
            tell(upper_in, me_wide - 1)

        @pl.when(me_wide == 1)
        def _():
            tell(lower_in, me_wide + 1)

    for c in range(ahead, chunks):
        stem(c)
        send_sub(c)
        to_slc(0, c - ahead)
    for c in range(chunks - ahead, chunks):
        to_slc(0, c)

    if n_wide > 2:
        @pl.when(me_wide <= n_wide - 3)
        def _():
            pl.semaphore_wait(upper_in, 1)

            @pl.when(me_wide >= 1)
            def _():
                tell(upper_in, me_wide - 1)

        @pl.when(me_wide >= 2)
        def _():
            pl.semaphore_wait(lower_in, 1)

            @pl.when(me_wide <= n_wide - 2)
            def _():
                tell(lower_in, me_wide + 1)

    for i in range(1, n_wide):
        for c in range(chunks):
            to_slc(i, c)

    positions = lax.broadcasted_iota(i32, (1, columns), 1)
    source = jnp.zeros((1, columns), i32)
    for j in range(col_bits):
        source = source + bit_of(positions, j) * lax.shift_left(jnp.int32(1), pick_ref[row_bits + col_bits + j])

    def build_columns(c):
        inner = lax.broadcasted_iota(i32, (width, columns), 0) + c * width
        col_mat[pl.ds(c * width, width), :] = sign_of(
            jnp.broadcast_to(source, (width, columns)), inner
        ).astype(jnp.bfloat16)

    def build_exit():
        legs = row_bits + col_bits
        scale = 0.5 ** (legs // 2) * (HALF_ROOT if legs % 2 else 1.0)
        place = lax.broadcasted_iota(i32, (n_wide * loc_pad, 1), 0)
        inner_loc = place & (loc_pad - 1)
        outer = lax.shift_right_logical(place, jnp.full_like(place, loc_pad.bit_length() - 1))
        end = vector_turns(outer, 0, wide_bits)
        end = end + vector_turns(inner_loc, row_bits - loc_bits, loc_bits)
        end = end + scalar_turns(me_group.astype(i32), wide_bits, group_bits)
        end = end + scalar_turns(me_wide.astype(i32), wide_bits + group_bits, rows_bits - loc_bits)
        end = end + vector_turns(source, row_bits, col_bits)
        out_cos[...] = turn_cos(end) * scale
        out_sin[...] = turn_sin(end) * scale

    for c in range(chunks):
        build_columns(c)
    for i in range(n_wide - 1):
        for c in range(chunks):
            to_wide(i, c)
    build_exit()
    for i in range(n_wide - 2):
        finish(i)
    finish(n_wide - 1)
    finish(n_wide - 2)
    blocks = butterfly([acc[w] for w in range(n_wide)])
    for w in range(n_wide):
        real, imag = blocks[w][:loc], blocks[w][loc_pad:loc_pad + loc]
        cos = out_cos[w * loc_pad:w * loc_pad + loc]
        sin = out_sin[w * loc_pad:w * loc_pad + loc]
        out_ref[0, w] = real * cos + imag * sin
        out_ref[1, w] = imag * cos - real * sin
    for copy in list(all_sub.values()) + list(all_slc.values()) + list(all_wide.values()):
        copy.wait_send()


def per_device(a_stem, b_stem, gate_pick, leg_order):
    columns = b_stem.shape[3]
    slices = a_stem.shape[1]
    bond = a_stem.shape[3]
    n_wide = lax.axis_size("wide")
    n_slc = lax.axis_size("slc")
    n_sub = lax.axis_size("sub")
    group = n_slc * n_sub
    rows_dev = a_stem.shape[2]
    rows_loc = rows_dev // group
    loc = rows_loc // n_wide
    loc_pad = max(loc, 8)
    width = 128
    chunks = columns // width
    dims = (n_sub, n_slc, n_wide, slices, rows_loc, loc, loc_pad, columns, width)
    f32, bf16 = jnp.float32, jnp.bfloat16
    tall = n_wide * loc_pad
    dma = pltpu.SemaphoreType.DMA
    block = (loc_pad, 2 * width)
    choices = jnp.concatenate((gate_pick, leg_order))
    out = pl.pallas_call(
        functools.partial(kernel_body, dims),
        out_shape=jax.ShapeDtypeStruct((2, n_wide, loc, columns), f32),
        in_specs=[pl.BlockSpec(memory_space=pltpu.HBM)] * 3,
        out_specs=pl.BlockSpec(memory_space=pltpu.VMEM),
        scratch_shapes=[
            pltpu.SMEM(choices.shape, jnp.int32),
            pltpu.VMEM((2, slices, rows_dev, bond), bf16),
            pltpu.VMEM((chunks, 2, slices, bond, width), bf16),
            pltpu.VMEM((group, rows_loc, 128), f32),
            pltpu.VMEM((group, rows_loc, 128), f32),
            pltpu.VMEM((tall, 2 * rows_loc), bf16),
            pltpu.VMEM((columns, columns), bf16),
            pltpu.VMEM((tall, columns), f32),
            pltpu.VMEM((tall, columns), f32),
            pltpu.VMEM((chunks, n_sub, n_slc, n_wide) + block, f32),
            pltpu.VMEM((chunks, n_sub - 1, n_slc, n_wide) + block, f32),
            pltpu.VMEM((n_wide, chunks, n_slc - 1) + block, f32),
            pltpu.VMEM((n_wide, chunks, n_slc - 1) + block, f32),
            pltpu.VMEM((n_wide, chunks) + block, f32),
            pltpu.VMEM((n_wide, chunks) + block, f32),
            pltpu.VMEM((n_wide, 2 * loc_pad, columns), f32),
            dma,
            dma,
            dma((chunks,)),
            dma((chunks, n_sub - 1, n_slc)),
            dma((chunks, n_sub - 1, n_slc)),
            dma((n_wide, chunks, n_slc - 1)),
            dma((n_wide, chunks, n_slc - 1)),
            dma((n_wide, chunks)),
            dma((n_wide, chunks)),
            pltpu.SemaphoreType.REGULAR,
            pltpu.SemaphoreType.REGULAR,
        ],
        compiler_params=pltpu.CompilerParams(
            collective_id=0, has_side_effects=True, vmem_limit_bytes=53 * 2**20
        ),
    )(choices, a_stem, b_stem)
    return out.reshape(2, n_wide, 1, 1, loc, columns)


def solution(mesh):
    placed = (
        P(None, ("grp", "slc", "sub"), "wide", None),
        P(None, ("grp", "slc", "sub"), None, None),
        P("grp"),
        P("grp"),
    )
    return jax.shard_map(
        per_device,
        mesh=mesh,
        in_specs=placed,
        out_specs=P(None, "grp", ("slc", "sub"), "wide", None, None),
        check_vma=False,
    )
```
